32 devices in a mesh: dp: 16 (over z, y, x), tensor: 2 (over core).
Axes of the slice: x: 2, y: 2, z: 4, core: 2. Of those that a mesh axis runs over, the one named last changes fastest.
Arguments:
- inputs: bfloat16 [16, 1024, 768], P(None, 'dp', 'tensor'), may hold values from -6 to 6
- lengths: int32 [16], replicated, may hold values from 1 to 1024, 12288 in all
- order: int32 [16], replicated, may hold values from 0 to 15, each once
- w_query: bfloat16 [768, 768], P(None, 'tensor'), may hold values from -0.3125 to 0.3125
- b_query: bfloat16 [768], P('tensor'), may hold values from -3 to 3
- w_key: bfloat16 [768, 768], P(None, 'tensor'), may hold values from -0.3125 to 0.3125
- w_value: bfloat16 [768, 768], P(None, 'tensor'), may hold values from -0.21875 to 0.21875
- b_value: bfloat16 [768], P('tensor'), may hold values from -3 to 3
- w_out: bfloat16 [768, 768], P('tensor'), may hold values from -0.875 to 0.875
- b_out: bfloat16 [768], P('tensor'), may hold values from -3 to 3
- gain_one: bfloat16 [768], P('tensor'), may hold values from 0.5 to 1.5
- shift_one: bfloat16 [768], P('tensor'), may hold values from -3 to 3
- w_up: bfloat16 [768, 3072], P(None, 'tensor'), may hold values from -0.21875 to 0.21875
- b_up: bfloat16 [3072], P('tensor'), may hold values from -3 to 3
- w_down: bfloat16 [3072, 768], P('tensor'), may hold values from -0.109375 to 0.109375
- b_down: bfloat16 [768], P('tensor'), may hold values from -3 to 3
- gain_two: bfloat16 [768], P('tensor'), may hold values from 0.5 to 1.5
- shift_two: bfloat16 [768], P('tensor'), may hold values from -3 to 3
- cotangent: bfloat16 [16, 1024, 768], P('dp', 'tensor'), may hold values from -6 to 6
Outputs:
- output: bfloat16 [16, 1024, 768], P('dp', 'tensor')
- input_grad: bfloat16 [16, 1024, 768], P(None, 'dp', 'tensor')
- grad_w_query: float32 [768, 768], P(None, 'tensor')
- grad_b_query: float32 [768], P('tensor')
- grad_w_key: float32 [768, 768], P(None, 'tensor')
- grad_w_value: float32 [768, 768], P(None, 'tensor')
- grad_b_value: float32 [768], P('tensor')
- grad_w_out: float32 [768, 768], P('tensor')
- grad_b_out: float32 [768], P('tensor')
- grad_gain_one: float32 [768], P('tensor')
- grad_shift_one: float32 [768], P('tensor')
- grad_w_up: float32 [768, 3072], P(None, 'tensor')
- grad_b_up: float32 [3072], P('tensor')
- grad_w_down: float32 [3072, 768], P('tensor')
- grad_b_down: float32 [768], P('tensor')
- grad_gain_two: float32 [768], P('tensor')
- grad_shift_two: float32 [768], P('tensor')
The draws below stay inside these ranges and needn't reach their ends.
Inputs may be any that keep to these rules, and one draw needn't show every extreme that they name: Valid tokens of each sequence; the first lengths entries of a sequence's 1024 slots hold its tokens, and some sequence fills all 1024. `order`: a permutation of the 16 sequences.
All inputs are finite; a program needn't handle non-finite values.
Results may differ from the reference program's by a relative error of at most 0.015.
The reference program's roundings to bfloat16 on the way count: a program that leaves them out, or rounds other values in their place, can miss the bound.
Values may be sent and summed in bfloat16 or wider, within the bound.
No kernel may reach another device: no remote copies, remote signals or barrier semaphores. Data moves between devices by JAX's collectives and lax.ppermute only.
A program may use at most 192 MiB of HBM per device.

```python
import math
import jax
import jax.numpy as jnp
import numpy as np
from jax import lax

D = 768
HEADS = 12
HEAD_DIM = 64
FF = 3072
SEQ_LEN = 1024
NUM_SEQS = 16
TOKENS = 16384


def steps_of(key, dims, split, smallest, high):
    level = 1.0
    for position, blocks in split:
        draws = jax.random.uniform(jax.random.fold_in(jax.random.fold_in(key, 6), position), (blocks,), jnp.float32, smallest / len(split), high / len(split))
        level = level * jnp.repeat(jnp.exp(draws), dims[position] // blocks).reshape((-1,) + (1,) * (len(dims) - 1 - position))
    return level


def length_profile(count, total, limit, skew):
    portions = [(1 << 20) // math.isqrt(grade ** skew) + 1 for grade in range(2, count + 1)]
    rest, given = total - limit - (count - 1), [1] * (count - 1)
    while rest > 0:
        movable = [i for i in range(count - 1) if given[i] < limit]
        whole, left = sum([portions[i] for i in movable]), rest
        for i in movable:
            more = min(limit - given[i], max(1, left * portions[i] // whole), rest)
            given[i] = given[i] + more
            rest = rest - more
    return np.array([limit] + given)


def uneven(stream_key, number_of, total, most, lean):
    if number_of == 2:
        one = jax.random.randint(stream_key, (), max(1, total - most), min(most, total - 1) + 1)
        return jnp.stack([one, total - one])
    sizes = jnp.asarray(length_profile(number_of, total, most, lean), jnp.int32)
    twos = (number_of - 1) // 2
    source_of, receiver = sizes[1:1 + 2 * twos:2], sizes[2:2 + 2 * twos:2]
    slack = jnp.minimum(source_of - 1, most - receiver)
    moved = jax.random.randint(jax.random.fold_in(stream_key, 1), (twos,), 0, 1 << 20) % (slack + 1)
    sizes = sizes.at[1:1 + 2 * twos:2].set(source_of - moved).at[2:2 + 2 * twos:2].set(receiver + moved)
    return sizes[jax.random.permutation(jax.random.fold_in(stream_key, 2), number_of)]


def centred(stream_key, extent, deviation, most, pieces=(), kind=jnp.bfloat16):
    entries = jax.random.normal(stream_key, extent, jnp.float32) * deviation
    if len(pieces) > 0:
        entries = steps_of(stream_key, extent, pieces, -0.22, 0.18) * entries
    return jnp.clip(entries, min=-most, max=most).astype(kind)


def setup_inputs(seed: int = 0) -> dict:
    streams_of = jax.random.split(jax.random.key(seed), 20)
    inputs = centred(streams_of[0], (NUM_SEQS, SEQ_LEN, D), 1.0, 6.0, ((1, 16), (2, 2)))
    lengths = uneven(streams_of[1], NUM_SEQS, NUM_SEQS * SEQ_LEN * 3 // 4, SEQ_LEN, 0).astype(jnp.int32)
    order = jax.random.permutation(streams_of[2], NUM_SEQS).astype(jnp.int32)
    w_query = centred(streams_of[3], (D, D), (D // 2) ** -0.5, 0.3125, ((1, 2),))
    b_query = centred(streams_of[4], (D,), 0.5, 3.0, ((0, 2),))
    w_key = centred(streams_of[5], (D, D), (D // 2) ** -0.5, 0.3125, ((1, 2),))
    w_value = centred(streams_of[6], (D, D), D ** -0.5, 0.21875, ((1, 2),))
    b_value = centred(streams_of[7], (D,), 0.5, 3.0, ((0, 2),))
    w_out = centred(streams_of[8], (D, D), (D // 16) ** -0.5, 0.875, ((0, 2),))
    b_out = centred(streams_of[9], (D,), 0.5, 3.0, ((0, 2),))
    gain_one = jnp.clip(1.0 + 0.1 * jax.random.normal(streams_of[10], (D,), jnp.float32), 0.5, 1.5).astype(jnp.bfloat16)
    shift_one = centred(streams_of[11], (D,), 0.5, 3.0, ((0, 2),))
    w_up = centred(streams_of[12], (D, FF), D ** -0.5, 0.21875, ((1, 2),))
    b_up = centred(streams_of[13], (FF,), 0.5, 3.0, ((0, 2),))
    w_down = centred(streams_of[14], (FF, D), FF ** -0.5, 0.109375, ((0, 2),))
    b_down = centred(streams_of[15], (D,), 0.5, 3.0, ((0, 2),))
    gain_two = jnp.clip(1.0 + 0.1 * jax.random.normal(streams_of[16], (D,), jnp.float32), 0.5, 1.5).astype(jnp.bfloat16)
    shift_two = centred(streams_of[17], (D,), 0.5, 3.0, ((0, 2),))
    cotangent = centred(streams_of[18], (NUM_SEQS, SEQ_LEN, D), 1.0, 6.0, ((0, 16), (1, 2)))
    return {"inputs": inputs, "lengths": lengths, "order": order, "w_query": w_query, "b_query": b_query, "w_key": w_key, "w_value": w_value, "b_value": b_value, "w_out": w_out, "b_out": b_out, "gain_one": gain_one, "shift_one": shift_one, "w_up": w_up, "b_up": b_up, "w_down": w_down, "b_down": b_down, "gain_two": gain_two, "shift_two": shift_two, "cotangent": cotangent}


epsilon = 1e-06

@jax.custom_vjp
def low(v):
    return lax.optimization_barrier(v.astype(jnp.bfloat16)).astype(jnp.float32)

@jax.custom_vjp
def low_back(v):
    return v

def low_keep(v):
    return (low(v), None)

def low_pass(kept, grad):
    return (grad,)

def back_keep(v):
    return (v, None)

def back_low(kept, grad):
    return (low(grad),)
low.defvjp(low_keep, low_pass)
low_back.defvjp(back_keep, back_low)

def matmul(left, right):
    return jnp.dot(left, right, precision=lax.Precision.HIGHEST)

def layer_norm(value, gain, shift):
    center = value - lax.optimization_barrier(jnp.mean(value, axis=-1, keepdims=True))
    spread = lax.optimization_barrier(jnp.mean(center * center, axis=-1, keepdims=True))
    return center * lax.rsqrt(spread + epsilon) * gain + shift

def attend(packed):
    query, keys, values, length = packed
    span = query.shape[0]
    query = query.reshape(span, HEADS, HEAD_DIM)
    keys = keys.reshape(span, HEADS, HEAD_DIM)
    values = values.reshape(span, HEADS, HEAD_DIM)
    raw = jnp.einsum('qhd,khd->hqk', query, keys, precision=lax.Precision.HIGHEST)
    scores = low_back(raw) * HEAD_DIM ** (-0.5)
    valid = jnp.arange(span) < length
    scores = jnp.where(valid[None, None, :], scores, -1e+30)
    probs = low(jax.nn.softmax(scores, axis=-1))
    mixed = jnp.einsum('hqk,khd->qhd', probs, values, precision=lax.Precision.HIGHEST)
    return mixed.reshape(span, HEADS * HEAD_DIM)

def encoder(params, block, block_lengths):
    w_query, b_query, w_key, w_value, b_value, w_out, b_out, gain_one, shift_one, w_up, b_up, w_down, b_down, gain_two, shift_two = params
    block_count, block_span, feature_width = block.shape
    block_shape = (block_count, block_span, feature_width)
    tokens_flat = block.reshape(block_count * block_span, feature_width)
    query = low(low_back(matmul(tokens_flat, w_query) + b_query))
    keys = low(low_back(matmul(tokens_flat, w_key)))
    values = low(low_back(matmul(tokens_flat, w_value) + b_value))
    mixed = lax.map(jax.checkpoint(attend), (query.reshape(block_shape), keys.reshape(block_shape), values.reshape(block_shape), block_lengths))
    mixed = low(low_back(mixed.reshape(block_count * block_span, feature_width)))
    attention = low_back(matmul(mixed, w_out)) + b_out
    normed = layer_norm(tokens_flat + attention, gain_one, shift_one)
    upper = low_back(matmul(low(normed), w_up)) + b_up
    active = low(jax.nn.gelu(upper, approximate=False))
    feed = low_back(matmul(active, w_down)) + b_down
    result = layer_norm(normed + feed, gain_two, shift_two)
    return result.reshape(block_shape)

def reference(inputs, lengths, order, w_query, b_query, w_key, w_value, b_value, w_out, b_out, gain_one, shift_one, w_up, b_up, w_down, b_down, gain_two, shift_two, cotangent):
    params = tuple((weight.astype(jnp.float32) for weight in (w_query, b_query, w_key, w_value, b_value, w_out, b_out, gain_one, shift_one, w_up, b_up, w_down, b_down, gain_two, shift_two)))
    dealt = inputs.astype(jnp.float32)[order]
    dealt_lengths = lengths[order]
    seq_total = dealt.shape[0]
    group = math.gcd(seq_total, max(1, 4096 // SEQ_LEN))
    groups = seq_total // group

    def group_step(carry, packed):
        block, block_lengths, block_cot = packed

        def forward(weights, values):
            return encoder(weights, values, block_lengths)
        result, pullback = jax.vjp(forward, params, block)
        weight_grads, block_grad = pullback(block_cot)
        carry = jax.tree.map(jnp.add, carry, weight_grads)
        return (carry, (result, block_grad))
    zeros = jax.tree.map(jnp.zeros_like, params)
    packed = (dealt.reshape(groups, group, SEQ_LEN, D), dealt_lengths.reshape(groups, group), cotangent.astype(jnp.float32).reshape(groups, group, SEQ_LEN, D))
    totals, (results, block_grads) = lax.scan(group_step, zeros, packed)
    output = results.reshape(seq_total, SEQ_LEN, D).astype(jnp.bfloat16)
    inverse = jnp.zeros((seq_total,), jnp.int32).at[order].set(jnp.arange(seq_total, dtype=jnp.int32))
    input_grad = block_grads.reshape(seq_total, SEQ_LEN, D)[inverse].astype(jnp.bfloat16)
    factor = TOKENS ** (-0.5)
    scaled = tuple((grad * factor for grad in totals))
    return (output, input_grad, scaled[0], scaled[1], scaled[2], scaled[3], scaled[4], scaled[5], scaled[6], scaled[7], scaled[8], scaled[9], scaled[10], scaled[11], scaled[12], scaled[13], scaled[14])
```

```python
import jax
import jax.numpy as jnp
from jax import lax
from jax.sharding import PartitionSpec as P

HEAD_DIM = 64
epsilon = 1e-06
masked_score = -1e30
f32 = jnp.float32
bf16 = jnp.bfloat16


def layer_norm(value, gain, shift):
    center = value - jnp.mean(value, axis=-1, keepdims=True)
    spread = jnp.mean(center * center, axis=-1, keepdims=True)
    return center * lax.rsqrt(spread + epsilon) * gain + shift


def gelu_exact(value):
    return jax.nn.gelu(value, approximate=False)


def product(left, right, form):
    return jnp.einsum(form, left, right, preferred_element_type=f32)


def masked_scores(query, keys, valid):
    scores = product(query, keys, "qhd,khd->hqk") * query.shape[-1] ** (-0.5)
    return jnp.where(valid[None, None, :], scores, masked_score)


def attend_forward(query, keys, values, valid):
    scores = masked_scores(query, keys, valid)
    top = jnp.max(scores, axis=-1, keepdims=True)
    weights = jnp.exp(scores - top)
    total = jnp.sum(weights, axis=-1, keepdims=True)
    probs_low = (weights / total).astype(bf16)
    mixed = product(probs_low, values, "hqk,khd->qhd")
    return mixed, (top + jnp.log(total))[..., 0]


def attend_backward(query, keys, values, valid, log_total, grad_mixed):
    scale = query.shape[-1] ** (-0.5)
    scores = masked_scores(query, keys, valid)
    probs = jnp.exp(scores - log_total[..., None])
    grad_values = product(probs.astype(bf16), grad_mixed, "hqk,qhd->khd")
    grad_probs = product(grad_mixed, values, "qhd,khd->hqk")
    inner = jnp.sum(grad_probs * probs, axis=-1, keepdims=True)
    grad_scores = (probs * (grad_probs - inner) * scale).astype(bf16)
    grad_query = product(grad_scores, keys, "hqk,khd->qhd")
    grad_keys = product(grad_scores, query, "hqk,qhd->khd")
    return grad_query, grad_keys, grad_values


def swap(value):
    return lax.ppermute(value, "tensor", [(0, 1), (1, 0)])


def across(value, bit):
    count = lax.axis_size("dp")
    return lax.ppermute(value, "dp", [(i, i ^ (1 << bit)) for i in range(count)])


def bit_of(bit):
    return (lax.axis_index("dp") >> bit) & 1


def bit_orders():
    bits = lax.axis_size("dp").bit_length() - 1
    plain = list(range(bits))
    other = [1, 0] + plain[2:]
    return plain, other


def scatter_sum(value, bits):
    for bit in bits:
        half = value.shape[0] // 2
        mine = bit_of(bit)
        away = lax.dynamic_slice_in_dim(value, (1 - mine) * half, half, 0).astype(bf16)
        kept = lax.dynamic_slice_in_dim(value, mine * half, half, 0)
        value = kept + across(away, bit).astype(f32)
    return value


def gather_back(value, bits):
    for bit in reversed(bits):
        mine = bit_of(bit)
        half = value.shape[0]
        got = across(value, bit)
        joined = jnp.zeros((2 * half,) + value.shape[1:], value.dtype)
        joined = lax.dynamic_update_slice_in_dim(joined, value, mine * half, 0)
        value = lax.dynamic_update_slice_in_dim(joined, got, (1 - mine) * half, 0)
    return value


def reduce_all(value, bits, factor):
    count = lax.axis_size("dp")
    rows, columns = value.shape
    parts = value.reshape(count, rows // count, columns)
    total = (scatter_sum(parts, bits) * factor).astype(bf16)
    return gather_back(total, bits).reshape(rows, columns).astype(f32)


def on_device(
    inputs,
    lengths,
    order,
    w_query,
    b_query,
    w_key,
    w_value,
    b_value,
    w_out,
    b_out,
    gain_one,
    shift_one,
    w_up,
    b_up,
    w_down,
    b_down,
    gain_two,
    shift_two,
    cotangent,
):
    dp_count = lax.axis_size("dp")
    seq_len = inputs.shape[1] * dp_count
    half = seq_len // 2
    side = lax.axis_index("tensor")
    width = w_query.shape[0]
    local_width = w_query.shape[1]
    local_heads = local_width // HEAD_DIM
    head_shape = (seq_len, local_heads, HEAD_DIM)
    factor = (order.shape[0] * seq_len) ** (-0.5)
    plain, other = bit_orders()

    def halves(value, axis):
        size = value.shape[axis] // 2
        mine = lax.dynamic_slice_in_dim(value, side * size, size, axis)
        theirs = lax.dynamic_slice_in_dim(value, (1 - side) * size, size, axis)
        return mine, theirs

    def ordered(mine, theirs, axis):
        return jnp.where(
            side == 0,
            jnp.concatenate([mine, theirs], axis),
            jnp.concatenate([theirs, mine], axis),
        )

    vectors = jnp.stack([b_out, gain_one, shift_one, b_down, gain_two, shift_two])
    vectors_full = ordered(vectors, swap(vectors), 1).astype(f32)
    bias_out, gain_first, shift_first, bias_down, gain_second, shift_second = [
        vectors_full[i] for i in range(6)
    ]
    dealt_half = lax.all_to_all(inputs[order], "dp", split_axis=0, concat_axis=1, tiled=True)[0]
    dealt = ordered(dealt_half, swap(dealt_half), 1)
    length = lengths[order][lax.axis_index("dp")]
    position = (jnp.arange(seq_len) + side * half) % seq_len
    valid = position < length
    own, rest = halves(dealt, 0)
    tokens = jnp.concatenate([own, rest], 0)

    query = (product(tokens, w_query, "nd,df->nf") + b_query.astype(f32)).astype(bf16)
    keys = product(tokens, w_key, "nd,df->nf").astype(bf16)
    values = (product(tokens, w_value, "nd,df->nf") + b_value.astype(f32)).astype(bf16)
    heads = [value.reshape(head_shape) for value in (query, keys, values)]
    mixed, log_total = attend_forward(*heads, valid)
    mixed = mixed.astype(bf16).reshape(seq_len, local_width)

    def join(terms_of):
        away = terms_of(1).astype(bf16)
        got = swap(away)
        return terms_of(0) + got.astype(f32)

    def rows_of(value, which):
        return value[which * half : (which + 1) * half]

    attention = join(lambda k: product(rows_of(mixed, k), w_out, "nh,hd->nd"))
    normed, norm_one_back = jax.vjp(
        layer_norm, own.astype(f32) + attention + bias_out, gain_first, shift_first
    )
    normed_low = normed.astype(bf16)
    normed_pair = [normed_low, swap(normed_low)]
    bias_up = b_up.astype(f32)
    active_pair, gelu_backs = [], []
    for part in normed_pair:
        upper = product(part, w_up, "nd,df->nf") + bias_up
        active, back = jax.vjp(gelu_exact, upper)
        active_pair.append(active.astype(bf16))
        gelu_backs.append(back)
    feed = join(lambda k: product(active_pair[k], w_down, "nf,fd->nd"))
    result, norm_two_back = jax.vjp(
        layer_norm, normed + feed + bias_down, gain_second, shift_second
    )
    output = result.astype(bf16)
    grad_two, grad_gain_two, grad_shift_two = norm_two_back(cotangent[0].astype(f32))
    grad_bias_down = jnp.sum(grad_two, axis=0)
    grad_two_low = grad_two.astype(bf16)
    grad_pair = [grad_two_low, swap(grad_two_low)]
    upper_pair, bias_up_terms = [], []
    for part, back in zip(grad_pair, gelu_backs):
        (grad_upper,) = back(product(part, w_down, "nd,fd->nf"))
        bias_up_terms.append(jnp.sum(grad_upper, axis=0))
        upper_pair.append(grad_upper.astype(bf16))
    grad_normed = join(lambda k: product(upper_pair[k], w_up, "nf,df->nd"))
    grad_w_down = product(
        jnp.concatenate(active_pair, 0), jnp.concatenate(grad_pair, 0), "nf,nd->fd"
    )
    down_sum = reduce_all(grad_w_down, plain, factor)
    grad_w_up = product(
        jnp.concatenate(normed_pair, 0), jnp.concatenate(upper_pair, 0), "nd,nf->df"
    )
    up_sum = reduce_all(grad_w_up, other, factor)
    grad_one, grad_gain_one, grad_shift_one = norm_one_back(grad_normed + grad_two)
    grad_bias_out = jnp.sum(grad_one, axis=0)
    grad_one_low = grad_one.astype(bf16)
    grad_one_all = jnp.concatenate([grad_one_low, swap(grad_one_low)], 0)
    grad_mixed = product(grad_one_all, w_out, "nd,hd->nh").astype(bf16)
    grad_w_out = product(mixed, grad_one_all, "nh,nd->hd")
    out_sum = reduce_all(grad_w_out, plain, factor)
    grad_query, grad_keys, grad_values = [
        value.astype(bf16).reshape(seq_len, local_width)
        for value in attend_backward(*heads, valid, log_total, grad_mixed.reshape(head_shape))
    ]

    def input_terms(which):
        pieces = [
            product(grad, halves(weight, 0)[which], "nf,df->nd")
            for grad, weight in (
                (grad_query, w_query),
                (grad_keys, w_key),
                (grad_values, w_value),
            )
        ]
        summed = pieces[0] + pieces[1] + pieces[2]
        straight = halves(grad_one, 1)[which]
        return jnp.concatenate([summed[:half] + straight, summed[half:]], 0)

    away = input_terms(1).astype(bf16)
    got = swap(away)
    kept = input_terms(0)
    grad_own = kept[:half] + got[half:].astype(f32)
    grad_rest = kept[half:] + got[:half].astype(f32)
    grad_inputs = ordered(grad_own.astype(bf16), grad_rest.astype(bf16), 0)[None]
    returned = lax.all_to_all(grad_inputs, "dp", split_axis=1, concat_axis=0, tiled=True)
    inverse = jnp.zeros_like(order).at[order].set(jnp.arange(order.shape[0], dtype=jnp.int32))
    input_grad = returned[inverse]

    grad_w_query = product(tokens, grad_query, "nd,nf->df")
    grad_w_key = product(tokens, grad_keys, "nd,nf->df")
    grad_w_value = product(tokens, grad_values, "nd,nf->df")
    query_sum = reduce_all(grad_w_query, plain, factor)
    key_sum = reduce_all(grad_w_key, other, factor)
    value_sum = reduce_all(grad_w_value, other, factor)

    vector_grads = jnp.stack(
        [
            grad_bias_out,
            grad_gain_one,
            grad_shift_one,
            grad_bias_down,
            grad_gain_two,
            grad_shift_two,
        ]
    )
    mine, theirs = halves(vector_grads, 1)
    mine = mine + swap(theirs)
    small = jnp.concatenate(
        [
            mine.reshape(-1),
            bias_up_terms[0] + bias_up_terms[1],
            jnp.sum(grad_query, axis=0, dtype=f32),
            jnp.sum(grad_values, axis=0, dtype=f32),
        ]
    ).reshape(-1, 128)
    for bit in plain:
        small = small + across(small, bit)
    small = (small * factor).reshape(-1)
    vector_sums = small[: 6 * local_width].reshape(6, local_width)
    b_up_sum = small[6 * local_width : 10 * local_width]
    b_query_sum = small[10 * local_width : 11 * local_width]
    b_value_sum = small[11 * local_width :]
    return (
        output[None],
        input_grad,
        query_sum,
        b_query_sum,
        key_sum,
        value_sum,
        b_value_sum,
        out_sum,
        vector_sums[0],
        vector_sums[1],
        vector_sums[2],
        up_sum,
        b_up_sum,
        down_sum,
        vector_sums[3],
        vector_sums[4],
        vector_sums[5],
    )


def solution(mesh):
    return jax.shard_map(
        on_device,
        mesh=mesh,
        in_specs=(
            P(None, "dp", "tensor"),
            P(),
            P(),
            P(None, "tensor"),
            P("tensor"),
            P(None, "tensor"),
            P(None, "tensor"),
            P("tensor"),
            P("tensor", None),
            P("tensor"),
            P("tensor"),
            P("tensor"),
            P(None, "tensor"),
            P("tensor"),
            P("tensor", None),
            P("tensor"),
            P("tensor"),
            P("tensor"),
            P("dp", "tensor", None),
        ),
        out_specs=(
            P("dp", "tensor", None),
            P(None, "dp", "tensor"),
            P(None, "tensor"),
            P("tensor"),
            P(None, "tensor"),
            P(None, "tensor"),
            P("tensor"),
            P("tensor", None),
            P("tensor"),
            P("tensor"),
            P("tensor"),
            P(None, "tensor"),
            P("tensor"),
            P("tensor", None),
            P("tensor"),
            P("tensor"),
            P("tensor"),
        ),
        check_vma=False,
    )
```

```python
import jax
import jax.numpy as jnp
from jax import lax
from jax.experimental import pallas as pl
from jax.experimental.pallas import tpu as pltpu
from jax.sharding import PartitionSpec as P

HEAD_DIM = 64
epsilon = 1e-06
masked_score = -1e30
f32 = jnp.float32
bf16 = jnp.bfloat16


def layer_norm(value, gain, shift):
    center = value - jnp.mean(value, axis=-1, keepdims=True)
    spread = jnp.mean(center * center, axis=-1, keepdims=True)
    return center * lax.rsqrt(spread + epsilon) * gain + shift


def gelu_exact(value):
    return jax.nn.gelu(value, approximate=False)


def product(left, right, form):
    return jnp.einsum(form, left, right, preferred_element_type=f32)


LANES = 128

def contract(left, right, left_axis, right_axis):
    return lax.dot_general(left, right, (((left_axis,), (right_axis,)), ((), ())), preferred_element_type=f32)

def only_head(value, head, axis):
    place = lax.broadcasted_iota(jnp.int32, value.shape, axis)
    return jnp.where((place // HEAD_DIM) == head, value, jnp.zeros_like(value))

def valid_rows(limits, shape):
    row = lax.broadcasted_iota(jnp.int32, shape, 0)
    return lax.rem(row + limits[1], shape[0]) < limits[0]

def forward_kernel(block, limits, query_ref, key_ref, value_ref, mixed_ref, total_ref):
    span = key_ref.shape[0]
    valid = valid_rows(limits, (span, block))
    values_t = value_ref[...].T
    head_keys = [only_head(key_ref[...], head, 1) for head in range(2)]
    for start in range(0, span, block):
        queries = query_ref[start:start + block, :] * jnp.asarray(HEAD_DIM ** -0.5, bf16)
        outs = []
        for head in range(2):
            scores = contract(head_keys[head], queries, 1, 1)
            scores = jnp.where(valid, scores, masked_score)
            top = jnp.max(scores, axis=0, keepdims=True)
            weights = jnp.exp(scores - top)
            total = jnp.sum(weights, axis=0, keepdims=True)
            out = contract(values_t[head * HEAD_DIM:(head + 1) * HEAD_DIM, :], weights.astype(bf16), 1, 0)
            outs.append(out / total)
            total_ref[0, head:head + 1, start:start + block] = top + jnp.log(total)
        mixed_ref[start:start + block, :] = jnp.concatenate(outs, 0).T.astype(bf16)

def attend_forward(query, keys, values, limits, block=256):
    span, width = query.shape
    pairs = width // LANES
    column = pl.BlockSpec((span, LANES), lambda i, limits: (0, i))
    return pl.pallas_call(
        lambda *refs: forward_kernel(block, *refs),
        out_shape=(jax.ShapeDtypeStruct((span, width), bf16), jax.ShapeDtypeStruct((pairs, 2, span), f32)),
        grid_spec=pltpu.PrefetchScalarGridSpec(
            num_scalar_prefetch=1, grid=(pairs,), in_specs=[column] * 3,
            out_specs=[column, pl.BlockSpec((1, 2, span), lambda i, limits: (i, 0, 0))]),
        cost_estimate=pl.CostEstimate(flops=16 * span * span * width, transcendentals=span * span * width // HEAD_DIM, bytes_accessed=8 * span * width),
        name="attend_forward",
    )(limits, query, keys, values)

def backward_kernel(block, limits, query_ref, key_ref, value_ref, grad_ref, total_ref, gq_ref, gk_ref, gv_ref, sum_k, sum_v):
    span = key_ref.shape[0]
    valid = valid_rows(limits, (span, block))
    scale = jnp.asarray(HEAD_DIM ** -0.5, bf16)
    keys_t = key_ref[...].T
    head_keys = [only_head(key_ref[...], head, 1) for head in range(2)]
    head_values = [only_head(value_ref[...], head, 1) for head in range(2)]
    for start in range(0, span, block):
        queries = query_ref[start:start + block, :] * scale
        grads = grad_ref[start:start + block, :]
        outs = []
        for head in range(2):
            scores = contract(head_keys[head], queries, 1, 1)
            probs = jnp.exp(scores - total_ref[0, head:head + 1, start:start + block])
            probs = jnp.where(valid, probs, 0.0)
            grad_probs = contract(head_values[head], grads, 1, 1)
            inner = jnp.sum(grad_probs * probs, axis=0, keepdims=True)
            grad_scores = (probs * (grad_probs - inner)).astype(bf16)
            more_v = contract(probs.astype(bf16), only_head(grads, head, 1), 1, 0)
            more_k = contract(grad_scores, only_head(queries, head, 1), 1, 0)
            if start == 0 and head == 0:
                sum_v[...] = more_v
                sum_k[...] = more_k
            else:
                sum_v[...] += more_v
                sum_k[...] += more_k
            outs.append(contract(keys_t[head * HEAD_DIM:(head + 1) * HEAD_DIM, :], grad_scores, 1, 0))
        gq_ref[start:start + block, :] = (jnp.concatenate(outs, 0).T * HEAD_DIM ** -0.5).astype(bf16)
    gk_ref[...] = sum_k[...].astype(bf16)
    gv_ref[...] = sum_v[...].astype(bf16)

def attend_backward(query, keys, values, limits, totals, grad_mixed, block=256, first=0, pairs=None):
    span, width = query.shape
    pairs = pairs or width // LANES
    column = pl.BlockSpec((span, LANES), lambda i, limits: (0, i + first))
    result = pl.BlockSpec((span, LANES), lambda i, limits: (0, i))
    shape = jax.ShapeDtypeStruct((span, pairs * LANES), bf16)
    return pl.pallas_call(
        lambda *refs: backward_kernel(block, *refs),
        out_shape=(shape,) * 3,
        grid_spec=pltpu.PrefetchScalarGridSpec(
            num_scalar_prefetch=1, grid=(pairs,),
            in_specs=[column] * 4 + [pl.BlockSpec((1, 2, span), lambda i, limits: (i + first, 0, 0))],
            out_specs=[result] * 3,
            scratch_shapes=[pltpu.VMEM((span, LANES), f32)] * 2),
        cost_estimate=pl.CostEstimate(flops=40 * span * span * pairs * LANES, transcendentals=span * span * pairs * 2, bytes_accessed=14 * span * pairs * LANES),
        name="attend_backward",
    )(limits, query, keys, values, grad_mixed, totals)


def swap(value):
    return lax.ppermute(value, "tensor", [(0, 1), (1, 0)])


def across(value, bit):
    count = lax.axis_size("dp")
    return lax.ppermute(value, "dp", [(i, i ^ (1 << bit)) for i in range(count)])


def bit_of(bit):
    return (lax.axis_index("dp") >> bit) & 1


def bit_orders():
    bits = lax.axis_size("dp").bit_length() - 1
    plain = list(range(bits))
    other = [1, 0] + plain[2:]
    return plain, other


def sent_half(value, bit):
    half = value.shape[0] // 2
    mine = bit_of(bit)
    away = lax.dynamic_slice_in_dim(value, (1 - mine) * half, half, 0).astype(bf16)
    kept = lax.dynamic_slice_in_dim(value, mine * half, half, 0)
    return kept, across(away, bit)


def scatter_sum(value, bits, after=()):
    after = list(after) + [None] * (len(bits) - len(after))
    for bit, other in zip(bits, after):
        kept, got = sent_half(value, bit)
        if other is not None:
            got, _ = lax.optimization_barrier((got, other))
        value = kept + got.astype(f32)
    return value


def gather_back(value, bits):
    for bit in reversed(bits[1:]):
        value = jnp.concatenate([value, across(value, bit)], 0)
    return value, across(value, bits[0])


def place_kernel(split, where, near_ref, far_ref, *out_refs):
    half = pl.num_programs(0) // 2
    from_far = (pl.program_id(0) ^ where[0]) >= half

    def put(source):
        for ref, piece in zip(out_refs, split(source[0])):
            ref[0] = piece.astype(f32)

    @pl.when(from_far)
    def _():
        put(far_ref)

    @pl.when(jnp.logical_not(from_far))
    def _():
        put(near_ref)


def place(near, far, bits, split, shapes):
    half, rows, columns = near.shape
    where = jnp.int32(0)
    for bit in bits:
        where = where * 2 + bit_of(bit)
    source = pl.BlockSpec((1, rows, columns), lambda j, where: ((j ^ where[0]) % half, 0, 0))
    return pl.pallas_call(
        lambda *refs: place_kernel(split, *refs),
        out_shape=[jax.ShapeDtypeStruct((2 * half,) + shape, f32) for shape in shapes],
        grid_spec=pltpu.PrefetchScalarGridSpec(
            num_scalar_prefetch=1,
            grid=(2 * half,),
            in_specs=[source, source],
            out_specs=[
                pl.BlockSpec((1,) + shape, lambda j, where: (j, 0, 0)) for shape in shapes
            ],
        ),
        cost_estimate=pl.CostEstimate(
            flops=0, transcendentals=0, bytes_accessed=16 * half * rows * columns
        ),
        name="place",
    )(where.reshape(1), near, far)


def whole(value):
    return [value]


def chunked(value):
    count = lax.axis_size("dp")
    return value.reshape(count, value.shape[0] // count, value.shape[1])


def reduce_all(parts, bits, factor, split, shapes, after=()):
    total = (scatter_sum(parts, bits, after) * factor).astype(bf16)
    near, far = gather_back(total, bits)
    return [
        value.reshape(-1, value.shape[-1]) for value in place(near, far, bits, split, shapes)
    ]


def on_device(
    inputs,
    lengths,
    order,
    w_query,
    b_query,
    w_key,
    w_value,
    b_value,
    w_out,
    b_out,
    gain_one,
    shift_one,
    w_up,
    b_up,
    w_down,
    b_down,
    gain_two,
    shift_two,
    cotangent,
):
    dp_count = lax.axis_size("dp")
    seq_len = inputs.shape[1] * dp_count
    half = seq_len // 2
    side = lax.axis_index("tensor")
    width = w_query.shape[0]
    local_width = w_query.shape[1]
    factor = (order.shape[0] * seq_len) ** (-0.5)
    plain, other = bit_orders()

    def halves(value, axis):
        size = value.shape[axis] // 2
        mine = lax.dynamic_slice_in_dim(value, side * size, size, axis)
        theirs = lax.dynamic_slice_in_dim(value, (1 - side) * size, size, axis)
        return mine, theirs

    def ordered(mine, theirs, axis):
        return jnp.where(
            side == 0,
            jnp.concatenate([mine, theirs], axis),
            jnp.concatenate([theirs, mine], axis),
        )

    vectors = jnp.stack([b_out, gain_one, shift_one, b_down, gain_two, shift_two])
    vectors_full = ordered(vectors, swap(vectors), 1).astype(f32)
    bias_out, gain_first, shift_first, bias_down, gain_second, shift_second = [
        vectors_full[i] for i in range(6)
    ]
    dealt_half = lax.all_to_all(inputs[order], "dp", split_axis=0, concat_axis=1, tiled=True)[0]
    dealt = ordered(dealt_half, swap(dealt_half), 1)
    length = lengths[order][lax.axis_index("dp")]
    limits = jnp.stack([length, side * half]).astype(jnp.int32)
    own, rest = halves(dealt, 0)
    tokens = jnp.concatenate([own, rest], 0)

    query = (product(tokens, w_query, "nd,df->nf") + b_query.astype(f32)).astype(bf16)
    keys = product(tokens, w_key, "nd,df->nf").astype(bf16)
    values = (product(tokens, w_value, "nd,df->nf") + b_value.astype(f32)).astype(bf16)
    mixed, log_total = attend_forward(query, keys, values, limits, seq_len)

    def join(terms_of):
        away = terms_of(1).astype(bf16)
        got = swap(away)
        return terms_of(0) + got.astype(f32)

    def rows_of(value, which):
        return value[which * half : (which + 1) * half]

    attention = join(lambda k: product(rows_of(mixed, k), w_out, "nh,hd->nd"))
    normed, norm_one_back = jax.vjp(
        layer_norm, own.astype(f32) + attention + bias_out, gain_first, shift_first
    )
    normed_low = normed.astype(bf16)
    normed_pair = [normed_low, swap(normed_low)]
    bias_up = b_up.astype(f32)
    active_pair, gelu_backs = [], []
    for part in normed_pair:
        upper = product(part, w_up, "nd,df->nf") + bias_up
        active, back = jax.vjp(gelu_exact, upper)
        active_pair.append(active.astype(bf16))
        gelu_backs.append(back)
    feed = join(lambda k: product(active_pair[k], w_down, "nf,fd->nd"))
    result, norm_two_back = jax.vjp(
        layer_norm, normed + feed + bias_down, gain_second, shift_second
    )
    output = result.astype(bf16)
    grad_two, grad_gain_two, grad_shift_two = norm_two_back(cotangent[0].astype(f32))
    grad_bias_down = jnp.sum(grad_two, axis=0)
    grad_two_low = grad_two.astype(bf16)
    grad_pair = [grad_two_low, swap(grad_two_low)]
    upper_pair, bias_up_terms = [], []
    for part, back in zip(grad_pair, gelu_backs):
        (grad_upper,) = back(product(part, w_down, "nd,fd->nf"))
        bias_up_terms.append(jnp.sum(grad_upper, axis=0))
        upper_pair.append(grad_upper.astype(bf16))
    grad_normed = join(lambda k: product(upper_pair[k], w_up, "nf,df->nd"))
    grad_w_down = product(
        jnp.concatenate(active_pair, 0), jnp.concatenate(grad_pair, 0), "nf,nd->fd"
    )
    grad_w_up = product(
        jnp.concatenate(normed_pair, 0), jnp.concatenate(upper_pair, 0), "nd,nf->df"
    )
    grad_one, grad_gain_one, grad_shift_one = norm_one_back(grad_normed + grad_two)
    grad_bias_out = jnp.sum(grad_one, axis=0)
    grad_one_low = grad_one.astype(bf16)
    grad_one_all = jnp.concatenate([grad_one_low, swap(grad_one_low)], 0)
    grad_mixed = product(grad_one_all, w_out, "nd,hd->nh").astype(bf16)
    grad_w_out = product(grad_one_all, mixed, "nd,nh->dh")
    pieces = [
        attend_backward(query, keys, values, limits, log_total, grad_mixed, half, first, 1)
        for first in range(local_width // LANES)
    ]
    (down_sum,) = reduce_all(
        chunked(grad_w_down), plain, factor, whole,
        [(grad_w_down.shape[0] // dp_count, width)],
        [piece[0] for piece in pieces[0::2]],
    )
    (up_sum,) = reduce_all(
        chunked(grad_w_up), other, factor, whole,
        [(width // dp_count, grad_w_up.shape[1])],
        [pieces[1][0]],
    )
    grad_query, grad_keys, grad_values = [
        jnp.concatenate([piece[i] for piece in pieces], 1) for i in range(3)
    ]

    def input_terms(which):
        pieces = [
            product(grad, halves(weight, 0)[which], "nf,df->nd")
            for grad, weight in (
                (grad_query, w_query),
                (grad_keys, w_key),
                (grad_values, w_value),
            )
        ]
        summed = pieces[0] + pieces[1] + pieces[2]
        straight = halves(grad_one, 1)[which]
        return jnp.concatenate([summed[:half] + straight, summed[half:]], 0)

    away = input_terms(1).astype(bf16)
    got = swap(away)
    kept = input_terms(0)
    grad_own = kept[:half] + got[half:].astype(f32)
    grad_rest = kept[half:] + got[:half].astype(f32)
    grad_inputs = ordered(grad_own.astype(bf16), grad_rest.astype(bf16), 0)
    grad_inputs = grad_inputs.reshape(dp_count, seq_len // dp_count, local_width)
    returned = lax.all_to_all(grad_inputs, "dp", split_axis=0, concat_axis=0, tiled=True)
    inverse = jnp.zeros_like(order).at[order].set(jnp.arange(order.shape[0], dtype=jnp.int32))
    input_grad = returned[inverse]

    grad_w_query = product(tokens, grad_query, "nd,nf->df")
    grad_w_both = product(tokens, jnp.concatenate([grad_keys, grad_values], 1), "nd,nf->df")
    chunk = width // dp_count
    shape = (chunk, local_width)
    query_sum, out_sum = reduce_all(
        jnp.concatenate([chunked(grad_w_query), chunked(grad_w_out)], 1), plain, factor,
        lambda value: [value[:chunk], value[chunk:]], [shape, shape],
    )
    out_sum = out_sum.T
    key_sum, value_sum = reduce_all(
        chunked(grad_w_both), other, factor,
        lambda value: [value[:, :local_width], value[:, local_width:]], [shape, shape],
    )

    vector_grads = jnp.stack(
        [
            grad_bias_out,
            grad_gain_one,
            grad_shift_one,
            grad_bias_down,
            grad_gain_two,
            grad_shift_two,
        ]
    )
    mine, theirs = halves(vector_grads, 1)
    mine = mine + swap(theirs)
    small = jnp.concatenate(
        [
            mine.reshape(-1),
            bias_up_terms[0] + bias_up_terms[1],
            jnp.sum(grad_query, axis=0, dtype=f32),
            jnp.sum(grad_values, axis=0, dtype=f32),
        ]
    ).reshape(-1, 128)
    for bit in plain:
        small = small + across(small, bit)
    small = (small * factor).reshape(-1)
    vector_sums = small[: 6 * local_width].reshape(6, local_width)
    b_up_sum = small[6 * local_width : 10 * local_width]
    b_query_sum = small[10 * local_width : 11 * local_width]
    b_value_sum = small[11 * local_width :]
    return (
        output[None],
        input_grad,
        query_sum,
        b_query_sum,
        key_sum,
        value_sum,
        b_value_sum,
        out_sum,
        vector_sums[0],
        vector_sums[1],
        vector_sums[2],
        up_sum,
        b_up_sum,
        down_sum,
        vector_sums[3],
        vector_sums[4],
        vector_sums[5],
    )


def solution(mesh):
    return jax.shard_map(
        on_device,
        mesh=mesh,
        in_specs=(
            P(None, "dp", "tensor"),
            P(),
            P(),
            P(None, "tensor"),
            P("tensor"),
            P(None, "tensor"),
            P(None, "tensor"),
            P("tensor"),
            P("tensor", None),
            P("tensor"),
            P("tensor"),
            P("tensor"),
            P(None, "tensor"),
            P("tensor"),
            P("tensor", None),
            P("tensor"),
            P("tensor"),
            P("tensor"),
            P("dp", "tensor", None),
        ),
        out_specs=(
            P("dp", "tensor", None),
            P(None, "dp", "tensor"),
            P(None, "tensor"),
            P("tensor"),
            P(None, "tensor"),
            P(None, "tensor"),
            P("tensor"),
            P("tensor", None),
            P("tensor"),
            P("tensor"),
            P("tensor"),
            P(None, "tensor"),
            P("tensor"),
            P("tensor", None),
            P("tensor"),
            P("tensor"),
            P("tensor"),
        ),
        check_vma=False,
    )
```
